32 devices in a mesh: section: 4 (over z), seq: 4 (over y, x), dp: 2 (over core).
Axes of the slice: x: 2, y: 2, z: 4, core: 2. Of those that a mesh axis runs over, the one named last changes fastest.
Arguments:
- inputs: bfloat16 [2, 2048, 512], P(None, 'dp', 'seq'), may hold values from -16 to 16, as said below
- filters: bfloat16 [4, 2, 1024, 512], P('section', 'dp', 'seq'), may hold values from -1 to 1
- norm_gain: float32 [4, 2048], P('section', 'dp'), may hold values from 0.25 to 1.75
- gate_weight: float32 [4, 2048], P('section', 'dp'), may hold values from -4 to 4
- gate_bias: float32 [4, 2048], P('section', 'dp'), may hold values from -4 to 4
- cotangents: bfloat16 [4, 2, 2048, 512], P('section', None, 'dp', 'seq'), may hold values from -2 to 2
Outputs:
- section_outputs: bfloat16 [4, 2, 2048, 512], P('section', None, 'dp', 'seq')
- gate_grads: float32 [4, 2, 2048], P('section', None, 'dp')
The draws below stay inside these ranges and needn't reach their ends.
Inputs may be any that keep to these rules, and one draw needn't show every extreme that they name: `inputs`: activations of order one.
All inputs are finite; a program needn't handle non-finite values.
Results may differ from the reference program's by a relative error of at most 0.008.
Values may be sent and summed in bfloat16 or wider, within the bound.
A program may use at most 64 MiB of HBM per device.

```python
import math
import jax
import jax.numpy as jnp
from jax import lax

D = 2048
MICRO = 2
SECTIONS = 4
LENGTH = 512
N_DP = 2


def draw_inputs(key, part):
    first_key = jax.random.fold_in(jax.random.fold_in(key, 11), 0)
    shape = (MICRO, D, LENGTH)
    base = jax.random.truncated_normal(first_key, -4.0, 4.0, shape, jnp.float32)
    channel_scale = jnp.sqrt(1.0 + 2.0 * jnp.arange(D, dtype=jnp.float32) / D)
    values = base * channel_scale[:, None]
    return values.astype(jnp.bfloat16)


def draw_filters(key, part):
    first_key, second_key = jax.random.split(jax.random.fold_in(key, 23), 2)
    shape = (SECTIONS, N_DP, D // N_DP, LENGTH)
    position = jnp.arange(LENGTH, dtype=jnp.float32) / LENGTH
    rates = jax.random.uniform(second_key, (SECTIONS, N_DP, D // N_DP, 1), jnp.float32, 0.0, 2.0)
    envelope = jnp.exp(-rates * position)
    scale = LENGTH ** (-0.5)
    base = jax.random.truncated_normal(first_key, -4.0, 4.0, shape, jnp.float32)
    values = scale * base * envelope
    return values.astype(jnp.bfloat16)


def draw_cotangents(key, part):
    first_key = jax.random.fold_in(jax.random.fold_in(key, 37), 0)
    shape = (SECTIONS, MICRO, D, LENGTH)
    position = jnp.arange(LENGTH, dtype=jnp.float32) / LENGTH
    scale = LENGTH ** (-0.5) * (1.0 + 2.0 * position)
    base = jax.random.truncated_normal(first_key, -4.0, 4.0, shape, jnp.float32)
    values = base * scale
    return values.astype(jnp.bfloat16)


def block_levels(key, shape, cuts, low, largest):
    def one(dim, parts):
        draws = jax.random.uniform(jax.random.fold_in(jax.random.fold_in(key, 6), dim), (parts,), jnp.float32, low / len(cuts), largest / len(cuts))
        return jnp.repeat(jnp.exp(draws), shape[dim] // parts).reshape((-1,) + (1,) * (len(shape) - dim - 1))

    level = one(*cuts[0])
    for cut in cuts[1:]:
        level = level * one(*cut)
    return level


def scatter_about(key, dims, spread, most, pieces=(), held_as=jnp.bfloat16):
    values = spread * jax.random.normal(key, dims, jnp.float32)
    if pieces:
        values = values * block_levels(key, dims, pieces, -0.22, 0.18)
    return jnp.clip(values, -most, most).astype(held_as)


def setup_inputs(seed: int = 0) -> dict:
    key_list = jax.random.split(jax.random.key(seed), 7)
    inputs = draw_inputs(jax.random.fold_in(key_list[6], 71), 0)
    filters = draw_filters(jax.random.fold_in(key_list[6], 71), 0)
    norm_gain = jnp.clip(1.0 + 0.15 * jax.random.normal(key_list[2], (SECTIONS, D), jnp.float32), 0.25, 1.75)
    gate_weight = scatter_about(key_list[3], (SECTIONS, D), 1.0, 4.0, ((0, 4), (1, 2)), jnp.float32)
    gate_bias = scatter_about(key_list[4], (SECTIONS, D), 1.0, 4.0, ((0, 4), (1, 2)), jnp.float32)
    cotangents = draw_cotangents(jax.random.fold_in(key_list[6], 71), 0)
    return {"inputs": inputs, "filters": filters, "norm_gain": norm_gain, "gate_weight": gate_weight, "gate_bias": gate_bias, "cotangents": cotangents}


EPS = 1e-06

def causal_conv(taps, signal):
    length = signal.shape[-1]
    spectrum = jnp.fft.rfft(taps, n=2 * length, axis=-1) * jnp.fft.rfft(signal, n=2 * length, axis=-1)
    return jnp.fft.irfft(spectrum, n=2 * length, axis=-1)[:, :length]

def blocked_conv(taps, signal):
    channels, length = signal.shape
    width = math.gcd(channels, 256)
    tap_blocks = taps.reshape(channels // width, width, length)
    sig_blocks = signal.reshape(channels // width, width, length)

    def single(pair):
        return causal_conv(pair[0], pair[1]).astype(jnp.bfloat16)
    return lax.map(single, (tap_blocks, sig_blocks)).reshape(channels, length)

def section_pass(values, taps, gain_row, weight_row, bias_row, cot_rows):
    values = values.astype(jnp.float32)
    mean_sq = lax.optimization_barrier(jnp.mean(values * values, axis=0))
    normed = values * lax.rsqrt(mean_sq + EPS)[None, :] * gain_row[:, None]
    normed_half = normed.astype(jnp.bfloat16)
    conv_half = blocked_conv(taps.astype(jnp.float32), normed_half.astype(jnp.float32))
    conv_full = conv_half.astype(jnp.float32)
    gate = jax.nn.sigmoid(weight_row[:, None] * normed + bias_row[:, None])
    result = (values + gate * conv_full).astype(jnp.bfloat16)
    slope = cot_rows.astype(jnp.float32) * conv_full * gate * (1.0 - gate)
    return (result, lax.optimization_barrier(jnp.sum(slope * normed, axis=1)), lax.optimization_barrier(jnp.sum(slope, axis=1)))

def reference(inputs, filters, norm_gain, gate_weight, gate_bias, cotangents):
    current = inputs
    outputs = []
    grads = []
    for section in range(SECTIONS):
        taps = filters[section].reshape(D, LENGTH)

        def single(pair, section=section, taps=taps):
            return section_pass(pair[0], taps, norm_gain[section], gate_weight[section], gate_bias[section], pair[1])
        result, grad_w, grad_b = lax.map(single, (current, cotangents[section]))
        current = result
        outputs.append(current)
        grads.append(jnp.stack([lax.optimization_barrier(jnp.sum(grad_w, axis=0)), lax.optimization_barrier(jnp.sum(grad_b, axis=0))]))
    return (jnp.stack(outputs), jnp.stack(grads))
```

```python
import functools

import jax
import jax.numpy as jnp
from jax import lax
from jax.experimental import pallas as pl
from jax.experimental.pallas import tpu as pltpu
from jax.sharding import PartitionSpec as P

EPS = 1e-06
MESH = pl.DeviceIdType.MESH
F32 = jnp.float32
BF16 = jnp.bfloat16


def kernel(
    sizes,
    inp, fil, cot, par,
    out, gout,
    xin, filr, parr, cotr, outb, gsend, psrc, pa, pbs, pb, msr,
    hs, toep, nrm, cnv, slp,
    xs, xr, fs, fr, rs, rr, cs, cr, ass, ar, bss, br, os_, or_, gs, gr, loc,
):
    n_z, n_q, n_d, micro, cw, pos, total = sizes
    rows = micro * n_q
    z = lax.axis_index("section")
    q = lax.axis_index("seq")
    d = lax.axis_index("dp")

    def remote(src, dst, ssem, rsem, zz, qq, dd):
        return pltpu.make_async_remote_copy(
            src_ref=src, dst_ref=dst, send_sem=ssem, recv_sem=rsem,
            device_id={"section": zz, "seq": qq, "dp": dd}, device_id_type=MESH,
        )

    def loop(n, body):
        lax.fori_loop(0, n, lambda i, c: (body(i), c)[1], 0)

    barrier = pltpu.get_barrier_semaphore()

    def greet(zz, qq, dd):
        pl.semaphore_signal(
            barrier, inc=1, device_id={"section": zz, "seq": qq, "dp": dd}, device_id_type=MESH
        )

    def greet_same(i):
        zz, qq = i // n_q, i % n_q

        @pl.when(jnp.logical_or(zz != z, qq != q))
        def _():
            greet(zz, qq, d)

    loop(n_z * n_q, greet_same)

    def greet_plane(i):
        qq, dd = i // n_d, i % n_d

        @pl.when(dd != d)
        def _():
            greet(z, qq, dd)

    loop(n_q * n_d, greet_plane)
    pl.semaphore_wait(barrier, n_z * n_q - 1 + n_q * (n_d - 1))

    def x_copy(peer, slot):
        return remote(inp.at[:, peer, z], xin.at[:, slot], xs.at[peer], xr.at[slot], z, peer, d)

    def f_copy(peer, slot):
        return remote(fil.at[peer], filr.at[slot], fs.at[peer], fr.at[slot], peer, q, d)

    def p_copy(peer, slot):
        return remote(par.at[peer], parr.at[slot], rs.at[peer], rr.at[slot], peer, q, d)

    def c_copy(pz, pq, sz, sq):
        return remote(
            cot.at[:, pq, pz], cotr.at[sz, :, sq], cs.at[pz, pq], cr.at[sz, sq], pz, pq, d
        )

    def each(n, me, body):
        def one(i):
            @pl.when(i != me)
            def _():
                body(i)

        loop(n, one)

    def each2(body):
        def one(i):
            zz, qq = i // n_q, i % n_q

            @pl.when(jnp.logical_or(zz != z, qq != q))
            def _():
                body(zz, qq)

        loop(n_z * n_q, one)

    each(n_q, q, lambda i: x_copy(i, q).start())
    each(n_z, z, lambda i: (p_copy(i, z).start(), f_copy(i, z).start())[0])
    own = [
        pltpu.make_async_copy(inp.at[:, q, z], xin.at[:, q], loc.at[0]),
        pltpu.make_async_copy(fil.at[z], filr.at[z], loc.at[1]),
        pltpu.make_async_copy(par.at[z], parr.at[z], loc.at[2]),
        pltpu.make_async_copy(cot.at[:, q, z], cotr.at[z, :, q], loc.at[3]),
    ]
    for c in own:
        c.start()
    for c in own:
        c.wait()
    each(n_q, q, lambda i: x_copy(i, i).wait_recv())
    each2(lambda zz, qq: c_copy(zz, qq, z, q).start())

    lane = lax.broadcasted_iota(jnp.int32, (cw, pos), 1)
    sub = lax.broadcasted_iota(jnp.int32, (cw, pos), 0)
    eye = lane == sub

    def column(row):
        return jnp.sum(jnp.where(eye, row, 0.0), axis=1, keepdims=True)

    def row_of(col):
        return jnp.sum(jnp.where(eye, col, 0.0), axis=0, keepdims=True)

    def squares(read):
        for r in range(rows):
            v = read(r).astype(F32)
            psrc[pl.ds(r, 1), :] = jnp.sum(v * v, axis=0, keepdims=True)

    def a_copy(pq, pd, sq, sd, par_):
        return remote(
            psrc, pa.at[par_, sq, sd], ass.at[par_, pq, pd], ar.at[par_, sq, sd], z, pq, pd
        )

    def each_plane(body):
        def one(i):
            qq, dd = i // n_d, i % n_d

            @pl.when(jnp.logical_or(dd != d, qq != q))
            def _():
                body(qq, dd)

        loop(n_q * n_d, one)

    def b_copy(pz, sz, par_):
        return remote(pbs, pb.at[par_, sz], bss.at[par_, pz], br.at[par_, sz], pz, q, d)

    tlane = lax.broadcasted_iota(jnp.int32, (16, pos), 1)
    tsub = lax.broadcasted_iota(jnp.int32, (16, pos), 0)
    groups = pos // 16

    def build(first, last):
        def one(c, carry):
            bases = []
            for k in range(n_q):
                h = hs[k, pl.ds(c, 1), :]
                wide = jnp.broadcast_to(h, (16, pos))
                bases.append(pltpu.roll(wide, 0, 1, stride=1, stride_axis=0).astype(BF16))
            for g in range(groups):
                before = jnp.zeros((16, pos), BF16)
                mask = tlane >= tsub + 16 * g
                for k in range(n_q):
                    now = bases[k] if g == 0 else pltpu.roll(bases[k], 16 * g, 1)
                    toep[c, k * pos + 16 * g : k * pos + 16 * g + 16, :] = jnp.where(
                        mask, now, before
                    )
                    before = now
            return carry

        lax.fori_loop(first, last, one, 0)

    block = lax.broadcasted_iota(jnp.int32, (rows, pos), 0) % n_q

    def convolve(c, carry):
        x = nrm[pl.ds(c, rows, stride=cw), :]
        parts = [x]
        for k in range(1, n_q):
            parts.append(jnp.where(block >= k, pltpu.roll(x, k, 0), 0.0))
        left = jnp.concatenate([p.astype(BF16) for p in parts], axis=1)
        cnv[pl.ds(c, rows, stride=cw), :] = jnp.dot(
            left, toep[c], preferred_element_type=F32
        )
        return carry

    half = max(cw // 2, 1)

    def exchange(s):
        par_ = s % 2
        each_plane(lambda qq, dd: a_copy(qq, dd, q, d, par_).start())
        pa[par_, q, d] = psrc[...]
        if s > 0:
            grads(s - 1)

        @pl.when(s != z)
        def _():
            f_copy(s, s).wait_recv()
            p_copy(s, s).wait_recv()

        for k in range(n_q):
            hs[k] = filr[s, :, k * pos : (k + 1) * pos].astype(F32)
        build(0, half)
        each_plane(lambda qq, dd: a_copy(qq, dd, qq, dd, par_).wait_recv())
        acc = pa[par_, 0, 0]
        for i in range(1, n_q * n_d):
            acc = acc + pa[par_, i // n_d, i % n_d]
        pbs[...] = acc
        each(n_z, z, lambda i: b_copy(i, z, par_).start())
        pb[par_, z] = acc
        build(half, cw)
        each(n_z, z, lambda i: b_copy(i, i, par_).wait_recv())
        acc = pb[par_, 0]
        for i in range(1, n_z):
            acc = acc + pb[par_, i]
        msr[...] = lax.rsqrt(acc / total + EPS)
        each_plane(lambda qq, dd: a_copy(qq, dd, q, d, par_).wait_send())
        each(n_z, z, lambda i: b_copy(i, z, par_).wait_send())

    def g_copy(pz, pq, sz, sq):
        return remote(
            gsend.at[pz], gout.at[sz, sq], gs.at[pz, pq], gr.at[sz, sq], pz, pq, d
        )

    def o_copy(pz, pq, sz, sq):
        return remote(
            outb.at[pz, :, pq], out.at[:, sq, sz], os_.at[pz, pq], or_.at[sz, sq], pz, pq, d
        )

    def grads(s):
        def arrive(i):
            @pl.when(jnp.logical_or(s != z, i != q))
            def _():
                c_copy(z, q, s, i).wait_recv()

        loop(n_q, arrive)
        acc_w = jnp.zeros((cw, pos), F32)
        acc_b = jnp.zeros((cw, pos), F32)
        for r in range(rows):
            slope = slp[pl.ds(r * cw, cw), :] * cotr[s, r // n_q, r % n_q].astype(F32)
            acc_w = acc_w + slope * nrm[pl.ds(r * cw, cw), :]
            acc_b = acc_b + slope
        gsend[s, 0:1, :] = row_of(jnp.sum(acc_w, axis=1, keepdims=True))
        gsend[s, 1:2, :] = row_of(jnp.sum(acc_b, axis=1, keepdims=True))

        def send(i):
            @pl.when(jnp.logical_or(s != z, i != q))
            def _():
                g_copy(s, i, z, q).start()

        loop(n_q, send)

        @pl.when(s == z)
        def _():
            gout[z, q] = gsend[s]

    for s in range(n_z):
        def read(r, s=s):
            a, b = r // n_q, r % n_q
            return xin[a, b] if s == 0 else outb[s - 1, a, b]

        squares(read)
        exchange(s)
        gain = column(parr[s, 0:1, :])
        weight = column(parr[s, 1:2, :])
        bias = column(parr[s, 2:3, :])
        for r in range(rows):
            nrm[pl.ds(r * cw, cw), :] = read(r).astype(F32) * msr[pl.ds(r, 1), :] * gain
        lax.fori_loop(0, cw, convolve, 0)
        for r in range(rows):
            span = pl.ds(r * cw, cw)
            conv = cnv[span, :].astype(BF16).astype(F32)
            gate = 1.0 / (1.0 + jnp.exp(-(weight * nrm[span, :] + bias)))
            outb[s, r // n_q, r % n_q] = (read(r).astype(F32) + gate * conv).astype(BF16)
            slp[span, :] = conv * gate * (1.0 - gate)

        def send(i, s=s):
            @pl.when(jnp.logical_or(s != z, i != q))
            def _():
                o_copy(s, i, z, q).start()

        loop(n_q, send)
    grads(n_z - 1)

    mine = pltpu.make_async_copy(outb.at[z, :, q], out.at[:, q, z], loc.at[0])
    mine.start()
    each(n_q, q, lambda i: x_copy(i, q).wait_send())
    each(n_z, z, lambda i: (p_copy(i, z).wait_send(), f_copy(i, z).wait_send())[0])
    each2(lambda zz, qq: c_copy(zz, qq, z, q).wait_send())
    each2(lambda zz, qq: o_copy(zz, qq, z, q).wait_send())
    each2(lambda zz, qq: g_copy(zz, qq, z, q).wait_send())
    each2(lambda zz, qq: o_copy(z, q, zz, qq).wait_recv())
    each2(lambda zz, qq: g_copy(z, q, zz, qq).wait_recv())
    mine.wait()


def local(inputs, filters, norm_gain, gate_weight, gate_bias, cotangents):
    n_z, n_q, n_d = (lax.axis_size(a) for a in ("section", "seq", "dp"))
    micro, channels, pos = inputs.shape
    length = filters.shape[-1]
    cw = channels // (n_q * n_z)
    rows = micro * n_q
    rank = lax.axis_index("seq")
    inp = inputs.reshape(micro, n_q, n_z, cw, pos)
    cot = cotangents.reshape(micro, n_q, n_z, cw, pos)
    fil = filters.reshape(n_z, cw, length)
    par = jnp.concatenate([norm_gain, gate_weight, gate_bias], axis=0)
    par = lax.dynamic_slice_in_dim(par.reshape(3, n_q, n_z, cw), rank, 1, 1)[:, 0]
    par = jnp.pad(par.transpose(1, 0, 2), ((0, 0), (0, 5), (0, pos - cw)))
    sizes = (n_z, n_q, n_d, micro, cw, pos, channels * n_d)
    dma = lambda *s: pltpu.SemaphoreType.DMA(s)
    vmem = pl.BlockSpec(memory_space=pltpu.VMEM)
    out, gout = pl.pallas_call(
        functools.partial(kernel, sizes),
        out_shape=(
            jax.ShapeDtypeStruct(inp.shape, BF16),
            jax.ShapeDtypeStruct((n_z, n_q, 8, pos), F32),
        ),
        in_specs=[vmem] * 4,
        out_specs=[vmem] * 2,
        scratch_shapes=[
            pltpu.VMEM((micro, n_q, cw, pos), BF16),
            pltpu.VMEM((n_z, cw, length), BF16),
            pltpu.VMEM((n_z, 8, pos), F32),
            pltpu.VMEM((n_z, micro, n_q, cw, pos), BF16),
            pltpu.VMEM((n_z, micro, n_q, cw, pos), BF16),
            pltpu.VMEM((n_z, 8, pos), F32),
            pltpu.VMEM((rows, pos), F32),
            pltpu.VMEM((2, n_q, n_d, rows, pos), F32),
            pltpu.VMEM((rows, pos), F32),
            pltpu.VMEM((2, n_z, rows, pos), F32),
            pltpu.VMEM((rows, pos), F32),
            pltpu.VMEM((n_q, cw, pos), F32),
            pltpu.VMEM((cw, length, pos), BF16),
            pltpu.VMEM((rows * cw, pos), F32),
            pltpu.VMEM((rows * cw, pos), F32),
            pltpu.VMEM((rows * cw, pos), F32),
            dma(n_q), dma(n_q), dma(n_z), dma(n_z), dma(n_z), dma(n_z),
            dma(n_z, n_q), dma(n_z, n_q),
            dma(2, n_q, n_d), dma(2, n_q, n_d), dma(2, n_z), dma(2, n_z),
            dma(n_z, n_q), dma(n_z, n_q), dma(n_z, n_q), dma(n_z, n_q),
            dma(4),
        ],
        compiler_params=pltpu.CompilerParams(
            collective_id=0, has_side_effects=True, vmem_limit_bytes=48 * 1024 * 1024
        ),
    )(inp, fil, cot, par)
    grads = gout[:, :, :2, :cw].transpose(2, 1, 0, 3).reshape(2, channels)
    return out.reshape(1, micro, channels, pos), grads[None]


def solution(mesh):
    return jax.shard_map(
        local,
        mesh=mesh,
        in_specs=(
            P(None, "dp", "seq"),
            P("section", "dp", "seq", None),
            P("section", "dp"),
            P("section", "dp"),
            P("section", "dp"),
            P("section", None, "dp", "seq"),
        ),
        out_specs=(P("section", None, "dp", "seq"), P("section", None, "dp")),
        check_vma=False,
    )
```

```python
import functools
import math

import jax
import jax.numpy as jnp
from jax import lax
from jax.experimental import pallas as pl
from jax.experimental.pallas import tpu as pltpu
from jax.sharding import PartitionSpec as P

EPS = 1e-06
MESH = pl.DeviceIdType.MESH
F32 = jnp.float32
BF16 = jnp.bfloat16


def kernel(
    sizes,
    inp, fil, cot, par,
    out, gout,
    xin, filr, parr, cotr, outb, gsend, psrc, pa, pbs, pb, msr,
    hs, toep, nrm, cnv, slp,
    xs, xr, fs, fr, rs, rr, cs, cr, ass, ar, bss, br, os_, or_, gs, gr, loc,
):
    n_z, n_q, n_d, micro, cw, pos, total = sizes
    rows = micro * n_q
    z = lax.axis_index("section")
    q = lax.axis_index("seq")
    d = lax.axis_index("dp")

    def remote(src, dst, ssem, rsem, zz, qq, dd):
        return pltpu.make_async_remote_copy(
            src_ref=src, dst_ref=dst, send_sem=ssem, recv_sem=rsem,
            device_id={"section": zz, "seq": qq, "dp": dd}, device_id_type=MESH,
        )

    def loop(n, body):
        lax.fori_loop(0, n, lambda i, c: (body(i), c)[1], 0)

    barrier = pltpu.get_barrier_semaphore()

    def greet(zz, qq, dd):
        pl.semaphore_signal(
            barrier, inc=1, device_id={"section": zz, "seq": qq, "dp": dd}, device_id_type=MESH
        )

    def greet_same(i):
        zz, qq = i // n_q, i % n_q

        @pl.when(jnp.logical_or(zz != z, qq != q))
        def _():
            greet(zz, qq, d)

    loop(n_z * n_q, greet_same)

    def greet_plane(i):
        qq, dd = i // n_d, i % n_d

        @pl.when(dd != d)
        def _():
            greet(z, qq, dd)

    loop(n_q * n_d, greet_plane)
    pl.semaphore_wait(barrier, n_z * n_q - 1 + n_q * (n_d - 1))

    def x_copy(peer, slot):
        return remote(inp.at[:, peer, z], xin.at[:, slot], xs.at[peer], xr.at[slot], z, peer, d)

    def f_copy(peer, slot):
        return remote(fil.at[peer], filr.at[slot], fs.at[peer], fr.at[slot], peer, q, d)

    def p_copy(peer, slot):
        return remote(par.at[peer], parr.at[slot], rs.at[peer], rr.at[slot], peer, q, d)

    def c_copy(pz, pq, sz, sq):
        return remote(
            cot.at[:, pq, pz], cotr.at[sz, :, sq], cs.at[pz, pq], cr.at[sz, sq], pz, pq, d
        )

    def each(n, me, body):
        def one(i):
            @pl.when(i != me)
            def _():
                body(i)

        loop(n, one)

    def each2(body):
        def one(i):
            zz, qq = i // n_q, i % n_q

            @pl.when(jnp.logical_or(zz != z, qq != q))
            def _():
                body(zz, qq)

        loop(n_z * n_q, one)

    each(n_q, q, lambda i: x_copy(i, q).start())
    each(n_z, z, lambda i: (p_copy(i, z).start(), f_copy(i, z).start())[0])
    own = [
        pltpu.make_async_copy(inp.at[:, q, z], xin.at[:, q], loc.at[0]),
        pltpu.make_async_copy(fil.at[z], filr.at[z], loc.at[1]),
        pltpu.make_async_copy(par.at[z], parr.at[z], loc.at[2]),
        pltpu.make_async_copy(cot.at[:, q, z], cotr.at[z, :, q], loc.at[3]),
    ]
    for c in own:
        c.start()
    for c in own:
        c.wait()
    each(n_q, q, lambda i: x_copy(i, i).wait_recv())

    lane = lax.broadcasted_iota(jnp.int32, (cw, pos), 1)
    sub = lax.broadcasted_iota(jnp.int32, (cw, pos), 0)
    eye = lane == sub

    def column(row):
        return jnp.sum(jnp.where(eye, row, 0.0), axis=1, keepdims=True)

    def row_of(col):
        return jnp.sum(jnp.where(eye, col, 0.0), axis=0, keepdims=True)

    def squares(read):
        for r in range(rows):
            v = read(r).astype(F32)
            psrc[pl.ds(r, 1), :] = jnp.sum(v * v, axis=0, keepdims=True)

    def a_copy(pq, pd, sq, sd, par_):
        return remote(
            psrc, pa.at[par_, sq, sd], ass.at[par_, pq, pd], ar.at[par_, sq, sd], z, pq, pd
        )

    def each_plane(body):
        def one(i):
            qq, dd = i // n_d, i % n_d

            @pl.when(jnp.logical_or(dd != d, qq != q))
            def _():
                body(qq, dd)

        loop(n_q * n_d, one)

    def b_copy(pz, sz, par_):
        return remote(pbs, pb.at[par_, sz], bss.at[par_, pz], br.at[par_, sz], pz, q, d)

    tlane = lax.broadcasted_iota(jnp.int32, (16, pos), 1)
    tsub = lax.broadcasted_iota(jnp.int32, (16, pos), 0)
    groups = pos // 16
    wide_by = math.gcd(cw, 8)

    def build(first, last):
        def one(c, carry):
            bases = []
            for k in range(n_q):
                h = hs[k, pl.ds(c, 1), :]
                wide = jnp.broadcast_to(h, (16, pos))
                bases.append(pltpu.roll(wide, 0, 1, stride=1, stride_axis=0).astype(BF16))
            for g in range(groups):
                before = jnp.zeros((16, pos), BF16)
                mask = tlane >= tsub + 16 * g
                for k in range(n_q):
                    now = bases[k] if g == 0 else pltpu.roll(bases[k], 16 * g, 1)
                    toep[c, k * pos + 16 * g : k * pos + 16 * g + 16, :] = jnp.where(
                        mask, now, before
                    )
                    before = now
            return carry

        lax.fori_loop(first, last, one, 0)

    block = lax.broadcasted_iota(jnp.int32, (rows, pos), 0) % n_q

    def convolve(i, carry, s=0):
        lefts = []
        for u in range(wide_by):
            x = nrm[s, pl.ds(i * wide_by + u, rows, stride=cw), :]
            parts = [x]
            for k in range(1, n_q):
                parts.append(jnp.where(block >= k, pltpu.roll(x, k, 0), 0.0))
            lefts.append(jnp.concatenate([p.astype(BF16) for p in parts], axis=1))
        sums = [
            jnp.dot(lefts[u], toep[i * wide_by + u], preferred_element_type=F32)
            for u in range(wide_by)
        ]
        for u in range(wide_by):
            cnv[pl.ds(i * wide_by + u, rows, stride=cw), :] = sums[u]
        return carry

    half = cw // 2

    def exchange(s):
        par_ = s % 2
        each_plane(lambda qq, dd: a_copy(qq, dd, q, d, par_).start())
        pa[par_, q, d] = psrc[...]
        if s > 1:
            grads(s - 2)

        @pl.when(s != z)
        def _():
            f_copy(s, s).wait_recv()
            p_copy(s, s).wait_recv()

        for k in range(n_q):
            hs[k] = filr[s, :, k * pos : (k + 1) * pos].astype(F32)
        build(0, half)
        each_plane(lambda qq, dd: a_copy(qq, dd, qq, dd, par_).wait_recv())
        acc = pa[par_, 0, 0]
        for i in range(1, n_q * n_d):
            acc = acc + pa[par_, i // n_d, i % n_d]
        pbs[...] = acc
        each(n_z, z, lambda i: b_copy(i, z, par_).start())
        pb[par_, z] = acc
        if s == 0:
            each2(lambda zz, qq: c_copy(zz, qq, z, q).start())
        else:
            send_out(s - 1)
        build(half, cw)
        each(n_z, z, lambda i: b_copy(i, i, par_).wait_recv())
        acc = pb[par_, 0]
        for i in range(1, n_z):
            acc = acc + pb[par_, i]
        msr[...] = lax.rsqrt(acc / total + EPS)
        each_plane(lambda qq, dd: a_copy(qq, dd, q, d, par_).wait_send())
        each(n_z, z, lambda i: b_copy(i, z, par_).wait_send())

    def g_copy(pz, pq, sz, sq):
        return remote(
            gsend.at[pz], gout.at[sz, sq], gs.at[pz, pq], gr.at[sz, sq], pz, pq, d
        )

    def o_copy(pz, pq, sz, sq):
        return remote(
            outb.at[pz, :, pq], out.at[:, sq, sz], os_.at[pz, pq], or_.at[sz, sq], pz, pq, d
        )

    def send_out(s):
        def send(i):
            @pl.when(jnp.logical_or(s != z, i != q))
            def _():
                o_copy(s, i, z, q).start()

        loop(n_q, send)

    def grads(s):
        def arrive(i):
            @pl.when(jnp.logical_or(s != z, i != q))
            def _():
                c_copy(z, q, s, i).wait_recv()

        loop(n_q, arrive)
        acc_w = jnp.zeros((cw, pos), F32)
        acc_b = jnp.zeros((cw, pos), F32)
        for r in range(rows):
            slope = slp[s, pl.ds(r * cw, cw), :] * cotr[s, r // n_q, r % n_q].astype(F32)
            acc_w = acc_w + slope * nrm[s, pl.ds(r * cw, cw), :]
            acc_b = acc_b + slope
        gsend[s, 0:1, :] = row_of(jnp.sum(acc_w, axis=1, keepdims=True))
        gsend[s, 1:2, :] = row_of(jnp.sum(acc_b, axis=1, keepdims=True))

        def send(i):
            @pl.when(jnp.logical_or(s != z, i != q))
            def _():
                g_copy(s, i, z, q).start()

        loop(n_q, send)

        @pl.when(s == z)
        def _():
            gout[z, q] = gsend[s]

    for s in range(n_z):
        def read(r, s=s):
            a, b = r // n_q, r % n_q
            return xin[a, b] if s == 0 else outb[s - 1, a, b]

        squares(read)
        exchange(s)
        gain = column(parr[s, 0:1, :])
        weight = column(parr[s, 1:2, :])
        bias = column(parr[s, 2:3, :])
        for r in range(rows):
            nrm[s, pl.ds(r * cw, cw), :] = read(r).astype(F32) * msr[pl.ds(r, 1), :] * gain
        lax.fori_loop(0, cw // wide_by, functools.partial(convolve, s=s), 0)
        for r in range(rows):
            span = pl.ds(r * cw, cw)
            conv = cnv[span, :].astype(BF16).astype(F32)
            gate = 1.0 / (1.0 + jnp.exp(-(weight * nrm[s, span, :] + bias)))
            outb[s, r // n_q, r % n_q] = (read(r).astype(F32) + gate * conv).astype(BF16)
            slp[s, span, :] = conv * gate * (1.0 - gate)

    send_out(n_z - 1)
    for s in range(max(n_z - 2, 0), n_z - 1):
        grads(s)
    grads(n_z - 1)

    mine = pltpu.make_async_copy(outb.at[z, :, q], out.at[:, q, z], loc.at[0])
    mine.start()
    each(n_q, q, lambda i: x_copy(i, q).wait_send())
    each(n_z, z, lambda i: (p_copy(i, z).wait_send(), f_copy(i, z).wait_send())[0])
    each2(lambda zz, qq: c_copy(zz, qq, z, q).wait_send())
    each2(lambda zz, qq: o_copy(zz, qq, z, q).wait_send())
    each2(lambda zz, qq: g_copy(zz, qq, z, q).wait_send())
    each2(lambda zz, qq: o_copy(z, q, zz, qq).wait_recv())
    each2(lambda zz, qq: g_copy(z, q, zz, qq).wait_recv())
    mine.wait()


def local(inputs, filters, norm_gain, gate_weight, gate_bias, cotangents):
    n_z, n_q, n_d = (lax.axis_size(a) for a in ("section", "seq", "dp"))
    micro, channels, pos = inputs.shape
    length = filters.shape[-1]
    cw = channels // (n_q * n_z)
    rows = micro * n_q
    rank = lax.axis_index("seq")
    inp = inputs.reshape(micro, n_q, n_z, cw, pos)
    cot = cotangents.reshape(micro, n_q, n_z, cw, pos)
    fil = filters.reshape(n_z, cw, length)
    par = jnp.concatenate([norm_gain, gate_weight, gate_bias], axis=0)
    par = lax.dynamic_slice_in_dim(par.reshape(3, n_q, n_z, cw), rank, 1, 1)[:, 0]
    par = jnp.pad(par.transpose(1, 0, 2), ((0, 0), (0, 5), (0, pos - cw)))
    sizes = (n_z, n_q, n_d, micro, cw, pos, channels * n_d)
    dma = lambda *s: pltpu.SemaphoreType.DMA(s)
    vmem = pl.BlockSpec(memory_space=pltpu.VMEM)
    out, gout = pl.pallas_call(
        functools.partial(kernel, sizes),
        out_shape=(
            jax.ShapeDtypeStruct(inp.shape, BF16),
            jax.ShapeDtypeStruct((n_z, n_q, 8, pos), F32),
        ),
        in_specs=[pl.BlockSpec(memory_space=pltpu.HBM)] * 3 + [vmem],
        out_specs=[vmem] * 2,
        scratch_shapes=[
            pltpu.VMEM((micro, n_q, cw, pos), BF16),
            pltpu.VMEM((n_z, cw, length), BF16),
            pltpu.VMEM((n_z, 8, pos), F32),
            pltpu.VMEM((n_z, micro, n_q, cw, pos), BF16),
            pltpu.VMEM((n_z, micro, n_q, cw, pos), BF16),
            pltpu.VMEM((n_z, 8, pos), F32),
            pltpu.VMEM((rows, pos), F32),
            pltpu.VMEM((2, n_q, n_d, rows, pos), F32),
            pltpu.VMEM((rows, pos), F32),
            pltpu.VMEM((2, n_z, rows, pos), F32),
            pltpu.VMEM((rows, pos), F32),
            pltpu.VMEM((n_q, cw, pos), F32),
            pltpu.VMEM((cw, length, pos), BF16),
            pltpu.VMEM((n_z, rows * cw, pos), F32),
            pltpu.VMEM((rows * cw, pos), F32),
            pltpu.VMEM((n_z, rows * cw, pos), F32),
            dma(n_q), dma(n_q), dma(n_z), dma(n_z), dma(n_z), dma(n_z),
            dma(n_z, n_q), dma(n_z, n_q),
            dma(2, n_q, n_d), dma(2, n_q, n_d), dma(2, n_z), dma(2, n_z),
            dma(n_z, n_q), dma(n_z, n_q), dma(n_z, n_q), dma(n_z, n_q),
            dma(4),
        ],
        compiler_params=pltpu.CompilerParams(
            collective_id=0, has_side_effects=True, vmem_limit_bytes=48 * 1024 * 1024
        ),
    )(inp, fil, cot, par)
    grads = gout[:, :, :2, :cw].transpose(2, 1, 0, 3).reshape(2, channels)
    return out.reshape(1, micro, channels, pos), grads[None]


def solution(mesh):
    return jax.shard_map(
        local,
        mesh=mesh,
        in_specs=(
            P(None, "dp", "seq"),
            P("section", "dp", "seq", None),
            P("section", "dp"),
            P("section", "dp"),
            P("section", "dp"),
            P("section", None, "dp", "seq"),
        ),
        out_specs=(P("section", None, "dp", "seq"), P("section", None, "dp")),
        check_vma=False,
    )
```

```python
import functools
import math

import jax
import jax.numpy as jnp
from jax import lax
from jax.experimental import pallas as pl
from jax.experimental.pallas import tpu as pltpu
from jax.sharding import PartitionSpec as P

EPS = 1e-06
MESH = pl.DeviceIdType.MESH
F32 = jnp.float32
BF16 = jnp.bfloat16


def kernel(
    sizes,
    inp, fil, cot, par,
    out, gout,
    xin, filr, parr, cotr, outb, gsend, psrc, pa, pbs, pb, msr,
    hs, toep, nrm, cnv, slp,
    xs, xr, fs, fr, rs, rr, cs, cr, ass, ar, bss, br, os_, or_, gs, gr, loc,
):
    n_z, n_q, n_d, micro, cw, pos, total = sizes
    rows = micro * n_q
    z = lax.axis_index("section")
    q = lax.axis_index("seq")
    d = lax.axis_index("dp")

    def remote(src, dst, ssem, rsem, zz, qq, dd):
        return pltpu.make_async_remote_copy(
            src_ref=src, dst_ref=dst, send_sem=ssem, recv_sem=rsem,
            device_id={"section": zz, "seq": qq, "dp": dd}, device_id_type=MESH,
        )

    def loop(n, body):
        lax.fori_loop(0, n, lambda i, c: (body(i), c)[1], 0)

    barrier = pltpu.get_barrier_semaphore()

    def greet(zz, qq, dd):
        pl.semaphore_signal(
            barrier, inc=1, device_id={"section": zz, "seq": qq, "dp": dd}, device_id_type=MESH
        )

    def greet_same(i):
        zz, qq = i // n_q, i % n_q

        @pl.when(jnp.logical_or(zz != z, qq != q))
        def _():
            greet(zz, qq, d)

    loop(n_z * n_q, greet_same)

    def greet_plane(i):
        qq, dd = i // n_d, i % n_d

        @pl.when(dd != d)
        def _():
            greet(z, qq, dd)

    loop(n_q * n_d, greet_plane)
    pl.semaphore_wait(barrier, n_z * n_q - 1 + n_q * (n_d - 1))

    def x_copy(peer, slot):
        return remote(inp.at[:, peer, z], xin.at[:, slot], xs.at[peer], xr.at[slot], z, peer, d)

    def f_copy(peer, slot):
        return remote(fil.at[peer], filr.at[slot], fs.at[peer], fr.at[slot], peer, q, d)

    def p_copy(peer, slot):
        return remote(par.at[peer], parr.at[slot], rs.at[peer], rr.at[slot], peer, q, d)

    def c_copy(pz, pq, sz, sq):
        return remote(
            cot.at[:, pq, pz], cotr.at[sz, :, sq], cs.at[pz, pq], cr.at[sz, sq], pz, pq, d
        )

    def each(n, me, body):
        def one(i):
            @pl.when(i != me)
            def _():
                body(i)

        loop(n, one)

    def each2(body):
        def one(i):
            zz, qq = i // n_q, i % n_q

            @pl.when(jnp.logical_or(zz != z, qq != q))
            def _():
                body(zz, qq)

        loop(n_z * n_q, one)

    each(n_q, q, lambda i: x_copy(i, q).start())
    each(n_z, z, lambda i: (p_copy(i, z).start(), f_copy(i, z).start())[0])
    own = [
        pltpu.make_async_copy(inp.at[:, q, z], xin.at[:, q], loc.at[0]),
        pltpu.make_async_copy(fil.at[z], filr.at[z], loc.at[1]),
        pltpu.make_async_copy(par.at[z], parr.at[z], loc.at[2]),
        pltpu.make_async_copy(cot.at[:, q, z], cotr.at[z, :, q], loc.at[3]),
    ]
    for c in own:
        c.start()
    for c in own:
        c.wait()
    each(n_q, q, lambda i: x_copy(i, i).wait_recv())

    lane = lax.broadcasted_iota(jnp.int32, (cw, pos), 1)
    sub = lax.broadcasted_iota(jnp.int32, (cw, pos), 0)
    eye = lane == sub

    def column(row):
        return jnp.sum(jnp.where(eye, row, 0.0), axis=1, keepdims=True)

    def row_of(col):
        return jnp.sum(jnp.where(eye, col, 0.0), axis=0, keepdims=True)

    def squares(read):
        for r in range(rows):
            v = read(r).astype(F32)
            psrc[pl.ds(r, 1), :] = jnp.sum(v * v, axis=0, keepdims=True)

    def a_copy(pq, pd, sq, sd, par_):
        return remote(
            psrc, pa.at[par_, sq, sd], ass.at[par_, pq, pd], ar.at[par_, sq, sd], z, pq, pd
        )

    def each_plane(body):
        def one(i):
            qq, dd = i // n_d, i % n_d

            @pl.when(jnp.logical_or(dd != d, qq != q))
            def _():
                body(qq, dd)

        loop(n_q * n_d, one)

    def b_copy(pz, sz, par_):
        return remote(pbs, pb.at[par_, sz], bss.at[par_, pz], br.at[par_, sz], pz, q, d)

    tlane = lax.broadcasted_iota(jnp.int32, (16, pos), 1)
    tsub = lax.broadcasted_iota(jnp.int32, (16, pos), 0)
    groups = pos // 16
    ahead = (tlane - tsub).astype(F32).astype(BF16)
    wide_by = math.gcd(cw, 8)

    def build(first, last):
        step_by = math.gcd(last - first, 4)

        def one(i, carry):
            for u in range(step_by):
                c = first + i * step_by + u
                bases = []
                for k in range(n_q):
                    wide = jnp.broadcast_to(hs[k, pl.ds(c, 1), :], (16, pos))
                    bases.append(pltpu.roll(wide, 0, 1, stride=1, stride_axis=0).astype(BF16))
                for g in range(groups):
                    before = jnp.zeros((16, pos), BF16)
                    mask = ahead >= 16.0 * g
                    for k in range(n_q):
                        now = bases[k] if g == 0 else pltpu.roll(bases[k], 16 * g, 1)
                        toep[c, k * pos + 16 * g : k * pos + 16 * g + 16, :] = jnp.where(
                            mask, now, before
                        )
                        before = now
            return carry

        lax.fori_loop(0, (last - first) // step_by, one, 0)

    block = lax.broadcasted_iota(jnp.int32, (rows, pos), 0) % n_q

    def convolve(i, carry, s=0):
        lefts = []
        for u in range(wide_by):
            x = nrm[s, pl.ds(i * wide_by + u, rows, stride=cw), :]
            parts = [x]
            for k in range(1, n_q):
                parts.append(jnp.where(block >= k, pltpu.roll(x, k, 0), 0.0))
            lefts.append(jnp.concatenate([p.astype(BF16) for p in parts], axis=1))
        sums = [
            jnp.dot(lefts[u], toep[i * wide_by + u], preferred_element_type=F32)
            for u in range(wide_by)
        ]
        for u in range(wide_by):
            cnv[pl.ds(i * wide_by + u, rows, stride=cw), :] = sums[u]
        return carry

    half = cw // 2

    def exchange(s):
        par_ = s % 2
        each_plane(lambda qq, dd: a_copy(qq, dd, q, d, par_).start())
        pa[par_, q, d] = psrc[...]
        if s > 1:
            grads(s - 2)

        @pl.when(s != z)
        def _():
            f_copy(s, s).wait_recv()
            p_copy(s, s).wait_recv()

        for k in range(n_q):
            hs[k] = filr[s, :, k * pos : (k + 1) * pos].astype(F32)
        build(0, half)
        each_plane(lambda qq, dd: a_copy(qq, dd, qq, dd, par_).wait_recv())
        acc = pa[par_, 0, 0]
        for i in range(1, n_q * n_d):
            acc = acc + pa[par_, i // n_d, i % n_d]
        pbs[...] = acc
        each(n_z, z, lambda i: b_copy(i, z, par_).start())
        pb[par_, z] = acc
        if s == 0:
            each2(lambda zz, qq: c_copy(zz, qq, z, q).start())
        else:
            send_out(s - 1)
        build(half, cw)
        each(n_z, z, lambda i: b_copy(i, i, par_).wait_recv())
        acc = pb[par_, 0]
        for i in range(1, n_z):
            acc = acc + pb[par_, i]
        msr[...] = lax.rsqrt(acc / total + EPS)
        each_plane(lambda qq, dd: a_copy(qq, dd, q, d, par_).wait_send())
        each(n_z, z, lambda i: b_copy(i, z, par_).wait_send())

    def g_copy(pz, pq, sz, sq):
        return remote(
            gsend.at[pz], gout.at[sz, sq], gs.at[pz, pq], gr.at[sz, sq], pz, pq, d
        )

    def o_copy(pz, pq, sz, sq):
        return remote(
            outb.at[pz, :, pq], out.at[:, sq, sz], os_.at[pz, pq], or_.at[sz, sq], pz, pq, d
        )

    def send_out(s):
        def send(i):
            @pl.when(jnp.logical_or(s != z, i != q))
            def _():
                o_copy(s, i, z, q).start()

        loop(n_q, send)

    def grads(s):
        def arrive(i):
            @pl.when(jnp.logical_or(s != z, i != q))
            def _():
                c_copy(z, q, s, i).wait_recv()

        loop(n_q, arrive)
        acc_w = jnp.zeros((cw, pos), F32)
        acc_b = jnp.zeros((cw, pos), F32)
        for r in range(rows):
            slope = slp[s, pl.ds(r * cw, cw), :] * cotr[s, r // n_q, r % n_q].astype(F32)
            acc_w = acc_w + slope * nrm[s, pl.ds(r * cw, cw), :]
            acc_b = acc_b + slope
        gsend[s, 0:1, :] = row_of(jnp.sum(acc_w, axis=1, keepdims=True))
        gsend[s, 1:2, :] = row_of(jnp.sum(acc_b, axis=1, keepdims=True))

        def send(i):
            @pl.when(jnp.logical_or(s != z, i != q))
            def _():
                g_copy(s, i, z, q).start()

        loop(n_q, send)

        @pl.when(s == z)
        def _():
            gout[z, q] = gsend[s]

    for s in range(n_z):
        def read(r, s=s):
            a, b = r // n_q, r % n_q
            return xin[a, b] if s == 0 else outb[s - 1, a, b]

        squares(read)
        exchange(s)
        gain = column(parr[s, 0:1, :])
        weight = column(parr[s, 1:2, :])
        bias = column(parr[s, 2:3, :])
        for r in range(rows):
            nrm[s, pl.ds(r * cw, cw), :] = read(r).astype(F32) * msr[pl.ds(r, 1), :] * gain
        lax.fori_loop(0, cw // wide_by, functools.partial(convolve, s=s), 0)
        for r in range(rows):
            span = pl.ds(r * cw, cw)
            conv = cnv[span, :].astype(BF16).astype(F32)
            gate = 1.0 / (1.0 + jnp.exp(-(weight * nrm[s, span, :] + bias)))
            outb[s, r // n_q, r % n_q] = (read(r).astype(F32) + gate * conv).astype(BF16)
            slp[s, span, :] = conv * gate * (1.0 - gate)

    send_out(n_z - 1)
    for s in range(max(n_z - 2, 0), n_z - 1):
        grads(s)
    grads(n_z - 1)

    mine = pltpu.make_async_copy(outb.at[z, :, q], out.at[:, q, z], loc.at[0])
    mine.start()
    each(n_q, q, lambda i: x_copy(i, q).wait_send())
    each(n_z, z, lambda i: (p_copy(i, z).wait_send(), f_copy(i, z).wait_send())[0])
    each2(lambda zz, qq: c_copy(zz, qq, z, q).wait_send())
    each2(lambda zz, qq: o_copy(zz, qq, z, q).wait_send())
    each2(lambda zz, qq: g_copy(zz, qq, z, q).wait_send())
    each2(lambda zz, qq: o_copy(z, q, zz, qq).wait_recv())
    each2(lambda zz, qq: g_copy(z, q, zz, qq).wait_recv())
    mine.wait()


def local(inputs, filters, norm_gain, gate_weight, gate_bias, cotangents):
    n_z, n_q, n_d = (lax.axis_size(a) for a in ("section", "seq", "dp"))
    micro, channels, pos = inputs.shape
    length = filters.shape[-1]
    cw = channels // (n_q * n_z)
    rows = micro * n_q
    rank = lax.axis_index("seq")
    inp = inputs.reshape(micro, n_q, n_z, cw, pos)
    cot = cotangents.reshape(micro, n_q, n_z, cw, pos)
    fil = filters.reshape(n_z, cw, length)
    par = jnp.concatenate([norm_gain, gate_weight, gate_bias], axis=0)
    par = lax.dynamic_slice_in_dim(par.reshape(3, n_q, n_z, cw), rank, 1, 1)[:, 0]
    par = jnp.pad(par.transpose(1, 0, 2), ((0, 0), (0, 5), (0, pos - cw)))
    sizes = (n_z, n_q, n_d, micro, cw, pos, channels * n_d)
    dma = lambda *s: pltpu.SemaphoreType.DMA(s)
    vmem = pl.BlockSpec(memory_space=pltpu.VMEM)
    out, gout = pl.pallas_call(
        functools.partial(kernel, sizes),
        out_shape=(
            jax.ShapeDtypeStruct(inp.shape, BF16),
            jax.ShapeDtypeStruct((n_z, n_q, 8, pos), F32),
        ),
        in_specs=[pl.BlockSpec(memory_space=pltpu.HBM)] * 3 + [vmem],
        out_specs=[vmem] * 2,
        scratch_shapes=[
            pltpu.VMEM((micro, n_q, cw, pos), BF16),
            pltpu.VMEM((n_z, cw, length), BF16),
            pltpu.VMEM((n_z, 8, pos), F32),
            pltpu.VMEM((n_z, micro, n_q, cw, pos), BF16),
            pltpu.VMEM((n_z, micro, n_q, cw, pos), BF16),
            pltpu.VMEM((n_z, 8, pos), F32),
            pltpu.VMEM((rows, pos), F32),
            pltpu.VMEM((2, n_q, n_d, rows, pos), F32),
            pltpu.VMEM((rows, pos), F32),
            pltpu.VMEM((2, n_z, rows, pos), F32),
            pltpu.VMEM((rows, pos), F32),
            pltpu.VMEM((n_q, cw, pos), F32),
            pltpu.VMEM((cw, length, pos), BF16),
            pltpu.VMEM((n_z, rows * cw, pos), F32),
            pltpu.VMEM((rows * cw, pos), F32),
            pltpu.VMEM((n_z, rows * cw, pos), F32),
            dma(n_q), dma(n_q), dma(n_z), dma(n_z), dma(n_z), dma(n_z),
            dma(n_z, n_q), dma(n_z, n_q),
            dma(2, n_q, n_d), dma(2, n_q, n_d), dma(2, n_z), dma(2, n_z),
            dma(n_z, n_q), dma(n_z, n_q), dma(n_z, n_q), dma(n_z, n_q),
            dma(4),
        ],
        compiler_params=pltpu.CompilerParams(
            collective_id=0, has_side_effects=True, vmem_limit_bytes=62 * 1024 * 1024
        ),
    )(inp, fil, cot, par)
    grads = gout[:, :, :2, :cw].transpose(2, 1, 0, 3).reshape(2, channels)
    return out.reshape(1, micro, channels, pos), grads[None]


def solution(mesh):
    return jax.shard_map(
        local,
        mesh=mesh,
        in_specs=(
            P(None, "dp", "seq"),
            P("section", "dp", "seq", None),
            P("section", "dp"),
            P("section", "dp"),
            P("section", "dp"),
            P("section", None, "dp", "seq"),
        ),
        out_specs=(P("section", None, "dp", "seq"), P("section", None, "dp")),
        check_vma=False,
    )
```

```python
import functools
import math

import jax
import jax.numpy as jnp
from jax import lax
from jax.experimental import pallas as pl
from jax.experimental.pallas import tpu as pltpu
from jax.sharding import PartitionSpec as P

EPS = 1e-06
MESH = pl.DeviceIdType.MESH
F32 = jnp.float32
BF16 = jnp.bfloat16


def kernel(
    sizes,
    inp, fil, cot, par,
    out, gout,
    xin, filr, parr, cotr, outb, gsend, psrc, pa, pbs, pb, msr,
    hs, cols, toep, nrm, cnv, slp,
    xs, xr, fs, fr, rs, rr, cs, cr, ass, ar, bss, br, os_, or_, gs, gr, ls, lr, loc,
):
    n_z, n_q, n_d, micro, cw, pos, total = sizes
    rows = micro * n_q
    z = lax.axis_index("section")
    q = lax.axis_index("seq")
    d = lax.axis_index("dp")

    def remote(src, dst, ssem, rsem, zz, qq, dd):
        return pltpu.make_async_remote_copy(
            src_ref=src, dst_ref=dst, send_sem=ssem, recv_sem=rsem,
            device_id={"section": zz, "seq": qq, "dp": dd}, device_id_type=MESH,
        )

    def loop(n, body, first=0):
        if n - first <= 16:
            for i in range(first, n):
                body(i)
        else:
            lax.fori_loop(first, n, lambda i, c: (body(i), c)[1], 0)

    barrier = pltpu.get_barrier_semaphore()

    def greet(zz, qq, dd):
        pl.semaphore_signal(
            barrier, inc=1, device_id={"section": zz, "seq": qq, "dp": dd}, device_id_type=MESH
        )

    def greet_same(i):
        zz, qq = i // n_q, i % n_q

        @pl.when(jnp.logical_or(zz != z, qq != q))
        def _():
            greet(zz, qq, d)

    loop(n_z * n_q, greet_same)

    def greet_plane(i):
        qq, dd = i // n_d, i % n_d

        @pl.when(dd != d)
        def _():
            greet(z, qq, dd)

    loop(n_q * n_d, greet_plane)
    pl.semaphore_wait(barrier, n_z * n_q - 1 + n_q * (n_d - 1))

    def x_copy(peer, slot):
        return remote(inp.at[:, peer, z], xin.at[:, slot], xs.at[peer], xr.at[slot], z, peer, d)

    def f_copy(peer, slot):
        return remote(fil.at[peer], filr.at[slot], fs.at[peer], fr.at[slot], peer, q, d)

    def p_copy(peer, slot):
        return remote(par.at[peer], parr.at[slot], rs.at[peer], rr.at[slot], peer, q, d)

    def c_copy(pz, pq, sz, sq):
        return remote(
            cot.at[:, pq, pz], cotr.at[sz, :, sq], cs.at[pz, pq], cr.at[sz, sq], pz, pq, d
        )

    def each(n, me, body):
        loop(n, lambda k: body(lax.rem(me + k, n)), 1)

    def each2(body):
        def one(k):
            peer = lax.rem(z * n_q + q + k, n_z * n_q)
            body(peer // n_q, lax.rem(peer, n_q))

        loop(n_z * n_q, one, 1)

    each(n_q, q, lambda i: x_copy(i, q).start())

    def send_filters():
        each(n_z, z, lambda i: (p_copy(i, z).start(), f_copy(i, z).start())[0])

    @pl.when(z == 0)
    def _():
        send_filters()

    own = [
        pltpu.make_async_copy(inp.at[:, q, z], xin.at[:, q], loc.at[0]),
        pltpu.make_async_copy(fil.at[z], filr.at[z], loc.at[1]),
        pltpu.make_async_copy(par.at[z], parr.at[z], loc.at[2]),
        pltpu.make_async_copy(cot.at[:, q, z], cotr.at[z, :, q], loc.at[3]),
    ]
    for c in own:
        c.start()
    for c in own:
        c.wait()
    each(n_q, q, lambda i: x_copy(i, i).wait_recv())

    lane = lax.broadcasted_iota(jnp.int32, (cw, pos), 1)
    sub = lax.broadcasted_iota(jnp.int32, (cw, pos), 0)
    eye = lane == sub

    def column(row):
        return jnp.sum(jnp.where(eye, row, 0.0), axis=1, keepdims=True)

    def row_of(col):
        return jnp.sum(jnp.where(eye, col, 0.0), axis=0, keepdims=True)

    def squares(read):
        for r in range(rows):
            v = read(r).astype(F32)
            psrc[pl.ds(r, 1), :] = jnp.sum(v * v, axis=0, keepdims=True)

    def a_copy(pq, pd, sq, sd, par_):
        return remote(
            psrc, pa.at[par_, sq, sd], ass.at[par_, pq, pd], ar.at[par_, sq, sd], z, pq, pd
        )

    def each_plane(body):
        def one(k):
            peer = lax.rem(q * n_d + d + k, n_q * n_d)
            body(peer // n_d, lax.rem(peer, n_d))

        loop(n_q * n_d, one, 1)

    def b_copy(pz, sz, par_):
        return remote(pbs, pb.at[par_, sz], bss.at[par_, pz], br.at[par_, sz], pz, q, d)

    tlane = lax.broadcasted_iota(jnp.int32, (16, pos), 1)
    tsub = lax.broadcasted_iota(jnp.int32, (16, pos), 0)
    groups = pos // 16
    ahead = (tlane - tsub).astype(F32).astype(BF16)
    wide_by = math.gcd(cw, 8)

    def build(first, last):
        step_by = math.gcd(last - first, 4)

        def one(i, carry):
            for u in range(step_by):
                c = first + i * step_by + u
                bases = []
                for k in range(n_q):
                    wide = jnp.broadcast_to(hs[k, pl.ds(c, 1), :], (16, pos))
                    bases.append(pltpu.roll(wide, 0, 1, stride=1, stride_axis=0).astype(BF16))
                for g in range(groups):
                    before = jnp.zeros((16, pos), BF16)
                    mask = ahead >= 16.0 * g
                    for k in range(n_q):
                        now = bases[k] if g == 0 else pltpu.roll(bases[k], 16 * g, 1)
                        toep[c, k * pos + 16 * g : k * pos + 16 * g + 16, :] = jnp.where(
                            mask, now, before
                        )
                        before = now
            return carry

        lax.fori_loop(0, (last - first) // step_by, one, 0)

    block = lax.broadcasted_iota(jnp.int32, (rows, pos), 0) % n_q

    def convolve(i, carry, s=0):
        lefts = []
        for u in range(wide_by):
            x = nrm[s, pl.ds(i * wide_by + u, rows, stride=cw), :]
            parts = [x]
            for k in range(1, n_q):
                parts.append(jnp.where(block >= k, pltpu.roll(x, k, 0), 0.0))
            lefts.append(jnp.concatenate([p.astype(BF16) for p in parts], axis=1))
        sums = [
            jnp.dot(lefts[u], toep[i * wide_by + u], preferred_element_type=F32)
            for u in range(wide_by)
        ]
        for u in range(wide_by):
            cnv[pl.ds(i * wide_by + u, rows, stride=cw), :] = sums[u]
        return carry

    half = cw // 2

    def exchange(s):
        par_ = s % 2
        each_plane(lambda qq, dd: a_copy(qq, dd, q, d, par_).start())
        pa[par_, q, d] = psrc[...]
        if s == 0:
            pl.when(z > 0)(send_filters)
        if s > 1:
            grads(s - 2)

        @pl.when(s != z)
        def _():
            f_copy(s, s).wait_recv()
            p_copy(s, s).wait_recv()

        for k in range(3):
            cols[k] = jnp.broadcast_to(column(parr[s, k : k + 1, :]), (cw, pos))
        for k in range(n_q):
            hs[k] = filr[s, :, k * pos : (k + 1) * pos].astype(F32)
        build(0, half)
        each_plane(lambda qq, dd: a_copy(qq, dd, qq, dd, par_).wait_recv())
        acc = pa[par_, 0, 0]
        for i in range(1, n_q * n_d):
            acc = acc + pa[par_, i // n_d, i % n_d]
        pbs[...] = acc
        each(n_z, z, lambda i: b_copy(i, z, par_).start())
        pb[par_, z] = acc
        if s > 0:
            send_out(s - 1)
        send_cot(s)
        build(half, cw)
        each(n_z, z, lambda i: b_copy(i, i, par_).wait_recv())
        acc = pb[par_, 0]
        for i in range(1, n_z):
            acc = acc + pb[par_, i]
        msr[...] = lax.rsqrt(acc / total + EPS)
        each_plane(lambda qq, dd: a_copy(qq, dd, q, d, par_).wait_send())
        each(n_z, z, lambda i: b_copy(i, z, par_).wait_send())

    def g_copy(pz, pq, sz, sq):
        return remote(
            gsend.at[pz], gout.at[sz, sq], gs.at[pz, pq], gr.at[sz, sq], pz, pq, d
        )

    def o_copy(pz, pq, sz, sq):
        return remote(
            outb.at[pz, :, pq], out.at[:, sq, sz], os_.at[pz, pq], or_.at[sz, sq], pz, pq, d
        )

    def piece_copy(piece, count, pz, pq, sz, sq):
        span = pl.ds(piece * (cw // count), cw // count)
        return remote(
            outb.at[pz, :, pq, span], out.at[:, sq, sz, span],
            ls.at[piece, pq], lr.at[piece, sz, sq], pz, pq, d,
        )

    def send_piece(s, piece, count):
        def send(i):
            @pl.when(jnp.logical_or(s != z, i != q))
            def _():
                piece_copy(piece, count, s, i, z, q).start()

        loop(n_q, send)

    def send_cot(slot):
        low = jnp.logical_or(2 * z < n_z, z == 0)
        late = jnp.where(low, z, z + 1)
        inner = jnp.logical_and(z > 0, z < n_z - 1)

        def one(zz, qq):
            longer = jnp.where(low, zz > z, zz < z)
            when = jnp.where(jnp.logical_and(inner, longer), late, 0)

            @pl.when(when == slot)
            def _():
                c_copy(zz, qq, z, q).start()

        each2(one)

    def send_out(s):
        def send(i):
            @pl.when(jnp.logical_or(s != z, i != q))
            def _():
                o_copy(s, i, z, q).start()

        loop(n_q, send)

    def grads(s):
        def arrive(i):
            @pl.when(jnp.logical_or(s != z, i != q))
            def _():
                c_copy(z, q, s, i).wait_recv()

        loop(n_q, arrive)
        acc_w = jnp.zeros((cw, pos), F32)
        acc_b = jnp.zeros((cw, pos), F32)
        for r in range(rows):
            slope = slp[s, pl.ds(r * cw, cw), :] * cotr[s, r // n_q, r % n_q].astype(F32)
            acc_w = acc_w + slope * nrm[s, pl.ds(r * cw, cw), :]
            acc_b = acc_b + slope
        gsend[s, 0:1, :] = row_of(jnp.sum(acc_w, axis=1, keepdims=True))
        gsend[s, 1:2, :] = row_of(jnp.sum(acc_b, axis=1, keepdims=True))

        def send(i):
            @pl.when(jnp.logical_or(s != z, i != q))
            def _():
                g_copy(s, i, z, q).start()

        loop(n_q, send)

        @pl.when(s == z)
        def _():
            gout[z, q] = gsend[s]

    for s in range(n_z):
        def read(r, s=s):
            a, b = r // n_q, r % n_q
            return xin[a, b] if s == 0 else outb[s - 1, a, b]

        squares(read)
        exchange(s)
        for r in range(rows):
            nrm[s, pl.ds(r * cw, cw), :] = read(r).astype(F32) * msr[pl.ds(r, 1), :] * cols[0]
        pieces = 1 if s < n_z - 1 else math.gcd(cw // 16, 2) if cw % 16 == 0 else 1
        part = cw // pieces
        for piece in range(pieces):
            first = piece * part
            lax.fori_loop(
                first // wide_by, (first + part) // wide_by, functools.partial(convolve, s=s), 0
            )
            inside = pl.ds(first, part)
            for r in range(rows):
                span = pl.ds(r * cw + first, part)
                a, b = r // n_q, r % n_q
                old = read(r).astype(F32) if pieces == 1 else outb[s - 1, a, b, inside].astype(F32)
                conv = cnv[span, :].astype(BF16).astype(F32)
                gate = 1.0 / (
                    1.0 + jnp.exp(-(cols[1, inside] * nrm[s, span, :] + cols[2, inside]))
                )
                outb[s, a, b, inside] = (old + gate * conv).astype(BF16)
                slp[s, span, :] = conv * gate * (1.0 - gate)
            if pieces > 1:
                send_piece(s, piece, pieces)
    if pieces == 1:
        send_out(n_z - 1)
    for s in range(max(n_z - 2, 0), n_z - 1):
        grads(s)
    grads(n_z - 1)

    mine = pltpu.make_async_copy(outb.at[z, :, q], out.at[:, q, z], loc.at[0])
    mine.start()
    each(n_q, q, lambda i: x_copy(i, q).wait_send())
    each(n_z, z, lambda i: (p_copy(i, z).wait_send(), f_copy(i, z).wait_send())[0])
    each2(lambda zz, qq: c_copy(zz, qq, z, q).wait_send())
    last = n_z - 1

    def out_sent(zz, qq):
        if pieces == 1:
            o_copy(zz, qq, z, q).wait_send()
            return

        @pl.when(zz != last)
        def _():
            o_copy(zz, qq, z, q).wait_send()

        @pl.when(zz == last)
        def _():
            for piece in range(pieces):
                piece_copy(piece, pieces, last, qq, z, q).wait_send()

    def out_came(zz, qq):
        if pieces == 1:
            o_copy(z, q, zz, qq).wait_recv()
            return

        @pl.when(z != last)
        def _():
            o_copy(z, q, zz, qq).wait_recv()

        @pl.when(z == last)
        def _():
            for piece in range(pieces):
                piece_copy(piece, pieces, last, q, zz, qq).wait_recv()

    each2(out_sent)
    each2(lambda zz, qq: g_copy(zz, qq, z, q).wait_send())
    each2(out_came)
    each2(lambda zz, qq: g_copy(z, q, zz, qq).wait_recv())
    mine.wait()


def local(inputs, filters, norm_gain, gate_weight, gate_bias, cotangents):
    n_z, n_q, n_d = (lax.axis_size(a) for a in ("section", "seq", "dp"))
    micro, channels, pos = inputs.shape
    length = filters.shape[-1]
    cw = channels // (n_q * n_z)
    rows = micro * n_q
    rank = lax.axis_index("seq")
    inp = inputs.reshape(micro, n_q, n_z, cw, pos)
    cot = cotangents.reshape(micro, n_q, n_z, cw, pos)
    fil = filters.reshape(n_z, cw, length)
    par = jnp.concatenate([norm_gain, gate_weight, gate_bias], axis=0)
    par = lax.dynamic_slice_in_dim(par.reshape(3, n_q, n_z, cw), rank, 1, 1)[:, 0]
    par = jnp.pad(par.transpose(1, 0, 2), ((0, 0), (0, 5), (0, pos - cw)))
    sizes = (n_z, n_q, n_d, micro, cw, pos, channels * n_d)
    dma = lambda *s: pltpu.SemaphoreType.DMA(s)
    vmem = pl.BlockSpec(memory_space=pltpu.VMEM)
    out, gout = pl.pallas_call(
        functools.partial(kernel, sizes),
        out_shape=(
            jax.ShapeDtypeStruct(inp.shape, BF16),
            jax.ShapeDtypeStruct((n_z, n_q, 8, pos), F32),
        ),
        in_specs=[pl.BlockSpec(memory_space=pltpu.HBM)] * 3 + [vmem],
        out_specs=[vmem] * 2,
        scratch_shapes=[
            pltpu.VMEM((micro, n_q, cw, pos), BF16),
            pltpu.VMEM((n_z, cw, length), BF16),
            pltpu.VMEM((n_z, 8, pos), F32),
            pltpu.VMEM((n_z, micro, n_q, cw, pos), BF16),
            pltpu.VMEM((n_z, micro, n_q, cw, pos), BF16),
            pltpu.VMEM((n_z, 8, pos), F32),
            pltpu.VMEM((rows, pos), F32),
            pltpu.VMEM((2, n_q, n_d, rows, pos), F32),
            pltpu.VMEM((rows, pos), F32),
            pltpu.VMEM((2, n_z, rows, pos), F32),
            pltpu.VMEM((rows, pos), F32),
            pltpu.VMEM((n_q, cw, pos), F32),
            pltpu.VMEM((3, cw, pos), F32),
            pltpu.VMEM((cw, length, pos), BF16),
            pltpu.VMEM((n_z, rows * cw, pos), F32),
            pltpu.VMEM((rows * cw, pos), F32),
            pltpu.VMEM((n_z, rows * cw, pos), F32),
            dma(n_q), dma(n_q), dma(n_z), dma(n_z), dma(n_z), dma(n_z),
            dma(n_z, n_q), dma(n_z, n_q),
            dma(2, n_q, n_d), dma(2, n_q, n_d), dma(2, n_z), dma(2, n_z),
            dma(n_z, n_q), dma(n_z, n_q), dma(n_z, n_q), dma(n_z, n_q),
            dma(2, n_q), dma(2, n_z, n_q), dma(4),
        ],
        compiler_params=pltpu.CompilerParams(
            collective_id=0, has_side_effects=True, vmem_limit_bytes=62 * 1024 * 1024
        ),
    )(inp, fil, cot, par)
    grads = gout[:, :, :2, :cw].transpose(2, 1, 0, 3).reshape(2, channels)
    return out.reshape(1, micro, channels, pos), grads[None]


def solution(mesh):
    return jax.shard_map(
        local,
        mesh=mesh,
        in_specs=(
            P(None, "dp", "seq"),
            P("section", "dp", "seq", None),
            P("section", "dp"),
            P("section", "dp"),
            P("section", "dp"),
            P("section", None, "dp", "seq"),
        ),
        out_specs=(P("section", None, "dp", "seq"), P("section", None, "dp")),
        check_vma=False,
    )
```

```python
import functools
import math

import jax
import jax.numpy as jnp
from jax import lax
from jax.experimental import pallas as pl
from jax.experimental.pallas import tpu as pltpu
from jax.sharding import PartitionSpec as P

EPS = 1e-06
MESH = pl.DeviceIdType.MESH
F32 = jnp.float32
BF16 = jnp.bfloat16


def kernel(
    sizes,
    inp, fil, cot, par,
    out, gout,
    xin, filr, parr, cotr, outb, gsend, psrc, pa, pbs, pb, msr,
    hs, cols, toep, nrm, cnv, slp,
    xs, xr, fs, fr, rs, rr, cs, cr, ass, ar, bss, br, os_, or_, gs, gr, ls, lr, loc,
):
    n_z, n_q, n_d, micro, cw, pos, total = sizes
    rows = micro * n_q
    z = lax.axis_index("section")
    q = lax.axis_index("seq")
    d = lax.axis_index("dp")

    def remote(src, dst, ssem, rsem, zz, qq, dd):
        return pltpu.make_async_remote_copy(
            src_ref=src, dst_ref=dst, send_sem=ssem, recv_sem=rsem,
            device_id={"section": zz, "seq": qq, "dp": dd}, device_id_type=MESH,
        )

    def loop(n, body, first=0):
        if n - first <= 16:
            for i in range(first, n):
                body(i)
        else:
            lax.fori_loop(first, n, lambda i, c: (body(i), c)[1], 0)

    barrier = pltpu.get_barrier_semaphore()

    def greet(zz, qq, dd):
        pl.semaphore_signal(
            barrier, inc=1, device_id={"section": zz, "seq": qq, "dp": dd}, device_id_type=MESH
        )

    def greet_same(i):
        zz, qq = i // n_q, i % n_q

        @pl.when(jnp.logical_or(zz != z, qq != q))
        def _():
            greet(zz, qq, d)

    loop(n_z * n_q, greet_same)

    def greet_plane(i):
        qq, dd = i // n_d, i % n_d

        @pl.when(dd != d)
        def _():
            greet(z, qq, dd)

    loop(n_q * n_d, greet_plane)
    pl.semaphore_wait(barrier, n_z * n_q - 1 + n_q * (n_d - 1))

    def x_copy(peer, slot):
        return remote(inp.at[:, peer, z], xin.at[:, slot], xs.at[peer], xr.at[slot], z, peer, d)

    def f_copy(peer, slot):
        return remote(fil.at[peer], filr.at[slot], fs.at[peer], fr.at[slot], peer, q, d)

    def p_copy(peer, slot):
        return remote(par.at[peer], parr.at[slot], rs.at[peer], rr.at[slot], peer, q, d)

    def c_copy(pz, pq, sz, sq):
        return remote(
            cot.at[:, pq, pz], cotr.at[sz, :, sq], cs.at[pz, pq], cr.at[sz, sq], pz, pq, d
        )

    def each(n, me, body):
        loop(n, lambda k: body(lax.rem(me + k, n)), 1)

    def each2(body):
        def one(k):
            peer = lax.rem(z * n_q + q + k, n_z * n_q)
            body(peer // n_q, lax.rem(peer, n_q))

        loop(n_z * n_q, one, 1)

    each(n_q, q, lambda i: x_copy(i, q).start())

    def send_filters():
        each(n_z, z, lambda i: (p_copy(i, z).start(), f_copy(i, z).start())[0])

    @pl.when(z == 0)
    def _():
        send_filters()

    own = [
        pltpu.make_async_copy(inp.at[:, q, z], xin.at[:, q], loc.at[0]),
        pltpu.make_async_copy(fil.at[z], filr.at[z], loc.at[1]),
        pltpu.make_async_copy(par.at[z], parr.at[z], loc.at[2]),
        pltpu.make_async_copy(cot.at[:, q, z], cotr.at[z, :, q], loc.at[3]),
    ]
    for c in own:
        c.start()
    for c in own:
        c.wait()
    each(n_q, q, lambda i: x_copy(i, i).wait_recv())

    lane = lax.broadcasted_iota(jnp.int32, (cw, pos), 1)
    sub = lax.broadcasted_iota(jnp.int32, (cw, pos), 0)
    eye = lane == sub

    def column(row):
        return jnp.sum(jnp.where(eye, row, 0.0), axis=1, keepdims=True)

    def row_of(col):
        return jnp.sum(jnp.where(eye, col, 0.0), axis=0, keepdims=True)

    def squares(read):
        for r in range(rows):
            v = read(r).astype(F32)
            psrc[pl.ds(r, 1), :] = jnp.sum(v * v, axis=0, keepdims=True)

    def a_copy(pq, pd, sq, sd, par_):
        return remote(
            psrc, pa.at[par_, sq, sd], ass.at[par_, pq, pd], ar.at[par_, sq, sd], z, pq, pd
        )

    def each_plane(body):
        def one(k):
            peer = lax.rem(q * n_d + d + k, n_q * n_d)
            body(peer // n_d, lax.rem(peer, n_d))

        loop(n_q * n_d, one, 1)

    def b_copy(pz, sz, par_):
        return remote(pbs, pb.at[par_, sz], bss.at[par_, pz], br.at[par_, sz], pz, q, d)

    tlane = lax.broadcasted_iota(jnp.int32, (16, pos), 1)
    tsub = lax.broadcasted_iota(jnp.int32, (16, pos), 0)
    groups = pos // 16
    ahead = (tlane - tsub).astype(F32).astype(BF16)
    wide_by = math.gcd(cw, 8)

    def build(first, last):
        step_by = math.gcd(last - first, 4)

        def one(i, carry):
            for u in range(step_by):
                c = first + i * step_by + u
                bases = []
                for k in range(n_q):
                    wide = jnp.broadcast_to(hs[k, pl.ds(c, 1), :], (16, pos))
                    bases.append(pltpu.roll(wide, 0, 1, stride=1, stride_axis=0).astype(BF16))
                for g in range(groups):
                    before = jnp.zeros((16, pos), BF16)
                    mask = ahead >= 16.0 * g
                    for k in range(n_q):
                        now = bases[k] if g == 0 else pltpu.roll(bases[k], 16 * g, 1)
                        toep[c, k * pos + 16 * g : k * pos + 16 * g + 16, :] = jnp.where(
                            mask, now, before
                        )
                        before = now
            return carry

        lax.fori_loop(0, (last - first) // step_by, one, 0)

    block = lax.broadcasted_iota(jnp.int32, (rows, pos), 0) % n_q

    def convolve(i, carry, s=0):
        lefts = []
        for u in range(wide_by):
            x = nrm[s, pl.ds(i * wide_by + u, rows, stride=cw), :]
            parts = [x]
            for k in range(1, n_q):
                parts.append(jnp.where(block >= k, pltpu.roll(x, k, 0), 0.0))
            lefts.append(jnp.concatenate([p.astype(BF16) for p in parts], axis=1))
        sums = [
            jnp.dot(lefts[u], toep[i * wide_by + u], preferred_element_type=F32)
            for u in range(wide_by)
        ]
        for u in range(wide_by):
            cnv[pl.ds(i * wide_by + u, rows, stride=cw), :] = sums[u]
        return carry

    half = cw // 2

    def exchange(s):
        par_ = s % 2
        each_plane(lambda qq, dd: a_copy(qq, dd, q, d, par_).start())
        pa[par_, q, d] = psrc[...]
        if s == 0:
            pl.when(z > 0)(send_filters)
        if s > 1:
            grads(s - 2)

        @pl.when(s != z)
        def _():
            f_copy(s, s).wait_recv()
            p_copy(s, s).wait_recv()

        for k in range(3):
            cols[k] = jnp.broadcast_to(column(parr[s, k : k + 1, :]), (cw, pos))
        for k in range(n_q):
            hs[k] = filr[s, :, k * pos : (k + 1) * pos].astype(F32)
        build(0, half)
        each_plane(lambda qq, dd: a_copy(qq, dd, qq, dd, par_).wait_recv())
        acc = pa[par_, 0, 0]
        for i in range(1, n_q * n_d):
            acc = acc + pa[par_, i // n_d, i % n_d]
        pbs[...] = acc
        each(n_z, z, lambda i: b_copy(i, z, par_).start())
        pb[par_, z] = acc
        if s > 0:
            send_out(s - 1)
        else:
            each2(lambda zz, qq: c_copy(zz, qq, z, q).start())
        build(half, cw)
        each(n_z, z, lambda i: b_copy(i, i, par_).wait_recv())
        acc = pb[par_, 0]
        for i in range(1, n_z):
            acc = acc + pb[par_, i]
        msr[...] = lax.rsqrt(acc / total + EPS)
        each_plane(lambda qq, dd: a_copy(qq, dd, q, d, par_).wait_send())
        each(n_z, z, lambda i: b_copy(i, z, par_).wait_send())

    def g_copy(pz, pq, sz, sq):
        return remote(
            gsend.at[pz], gout.at[sz, sq], gs.at[pz, pq], gr.at[sz, sq], pz, pq, d
        )

    def o_copy(pz, pq, sz, sq):
        return remote(
            outb.at[pz, :, pq], out.at[:, sq, sz], os_.at[pz, pq], or_.at[sz, sq], pz, pq, d
        )

    def piece_copy(piece, count, pz, pq, sz, sq):
        span = pl.ds(piece * (cw // count), cw // count)
        return remote(
            outb.at[pz, :, pq, span], out.at[:, sq, sz, span],
            ls.at[piece, pq], lr.at[piece, sz, sq], pz, pq, d,
        )

    def send_piece(s, piece, count):
        def send(i):
            @pl.when(jnp.logical_or(s != z, i != q))
            def _():
                piece_copy(piece, count, s, i, z, q).start()

        loop(n_q, send)

    def send_out(s):
        def send(i):
            @pl.when(jnp.logical_or(s != z, i != q))
            def _():
                o_copy(s, i, z, q).start()

        loop(n_q, send)

    def grads(s):
        def arrive(i):
            @pl.when(jnp.logical_or(s != z, i != q))
            def _():
                c_copy(z, q, s, i).wait_recv()

        loop(n_q, arrive)
        acc_w = jnp.zeros((cw, pos), F32)
        acc_b = jnp.zeros((cw, pos), F32)
        for r in range(rows):
            slope = slp[s, pl.ds(r * cw, cw), :] * cotr[s, r // n_q, r % n_q].astype(F32)
            acc_w = acc_w + slope * nrm[s, pl.ds(r * cw, cw), :]
            acc_b = acc_b + slope
        gsend[s, 0:1, :] = row_of(jnp.sum(acc_w, axis=1, keepdims=True))
        gsend[s, 1:2, :] = row_of(jnp.sum(acc_b, axis=1, keepdims=True))

        def send(i):
            @pl.when(jnp.logical_or(s != z, i != q))
            def _():
                g_copy(s, i, z, q).start()

        loop(n_q, send)

        @pl.when(s == z)
        def _():
            gout[z, q] = gsend[s]

    for s in range(n_z):
        def read(r, s=s):
            a, b = r // n_q, r % n_q
            return xin[a, b] if s == 0 else outb[s - 1, a, b]

        squares(read)
        exchange(s)
        for r in range(rows):
            nrm[s, pl.ds(r * cw, cw), :] = read(r).astype(F32) * msr[pl.ds(r, 1), :] * cols[0]
        pieces = 1 if s < n_z - 1 else math.gcd(cw // 16, 2) if cw % 16 == 0 else 1
        part = cw // pieces
        for piece in range(pieces):
            first = piece * part
            lax.fori_loop(
                first // wide_by, (first + part) // wide_by, functools.partial(convolve, s=s), 0
            )
            inside = pl.ds(first, part)
            for r in range(rows):
                span = pl.ds(r * cw + first, part)
                a, b = r // n_q, r % n_q
                old = read(r).astype(F32) if pieces == 1 else outb[s - 1, a, b, inside].astype(F32)
                conv = cnv[span, :].astype(BF16).astype(F32)
                gate = 1.0 / (
                    1.0 + jnp.exp(-(cols[1, inside] * nrm[s, span, :] + cols[2, inside]))
                )
                outb[s, a, b, inside] = (old + gate * conv).astype(BF16)
                slp[s, span, :] = conv * gate * (1.0 - gate)
            if pieces > 1:
                send_piece(s, piece, pieces)
    if pieces == 1:
        send_out(n_z - 1)
    for s in range(max(n_z - 2, 0), n_z - 1):
        grads(s)
    grads(n_z - 1)

    mine = pltpu.make_async_copy(outb.at[z, :, q], out.at[:, q, z], loc.at[0])
    mine.start()
    each(n_q, q, lambda i: x_copy(i, q).wait_send())
    each(n_z, z, lambda i: (p_copy(i, z).wait_send(), f_copy(i, z).wait_send())[0])
    each2(lambda zz, qq: c_copy(zz, qq, z, q).wait_send())
    last = n_z - 1

    def out_sent(zz, qq):
        if pieces == 1:
            o_copy(zz, qq, z, q).wait_send()
            return

        @pl.when(zz != last)
        def _():
            o_copy(zz, qq, z, q).wait_send()

        @pl.when(zz == last)
        def _():
            for piece in range(pieces):
                piece_copy(piece, pieces, last, qq, z, q).wait_send()

    def out_came(zz, qq):
        if pieces == 1:
            o_copy(z, q, zz, qq).wait_recv()
            return

        @pl.when(z != last)
        def _():
            o_copy(z, q, zz, qq).wait_recv()

        @pl.when(z == last)
        def _():
            for piece in range(pieces):
                piece_copy(piece, pieces, last, q, zz, qq).wait_recv()

    each2(out_sent)
    each2(lambda zz, qq: g_copy(zz, qq, z, q).wait_send())
    each2(out_came)
    each2(lambda zz, qq: g_copy(z, q, zz, qq).wait_recv())
    mine.wait()


def local(inputs, filters, norm_gain, gate_weight, gate_bias, cotangents):
    n_z, n_q, n_d = (lax.axis_size(a) for a in ("section", "seq", "dp"))
    micro, channels, pos = inputs.shape
    length = filters.shape[-1]
    cw = channels // (n_q * n_z)
    rows = micro * n_q
    rank = lax.axis_index("seq")
    inp = inputs.reshape(micro, n_q, n_z, cw, pos)
    cot = cotangents.reshape(micro, n_q, n_z, cw, pos)
    fil = filters.reshape(n_z, cw, length)
    par = jnp.concatenate([norm_gain, gate_weight, gate_bias], axis=0)
    par = lax.dynamic_slice_in_dim(par.reshape(3, n_q, n_z, cw), rank, 1, 1)[:, 0]
    par = jnp.pad(par.transpose(1, 0, 2), ((0, 0), (0, 5), (0, pos - cw)))
    sizes = (n_z, n_q, n_d, micro, cw, pos, channels * n_d)
    dma = lambda *s: pltpu.SemaphoreType.DMA(s)
    vmem = pl.BlockSpec(memory_space=pltpu.VMEM)
    out, gout = pl.pallas_call(
        functools.partial(kernel, sizes),
        out_shape=(
            jax.ShapeDtypeStruct(inp.shape, BF16),
            jax.ShapeDtypeStruct((n_z, n_q, 8, pos), F32),
        ),
        in_specs=[pl.BlockSpec(memory_space=pltpu.HBM)] * 3 + [vmem],
        out_specs=[vmem] * 2,
        scratch_shapes=[
            pltpu.VMEM((micro, n_q, cw, pos), BF16),
            pltpu.VMEM((n_z, cw, length), BF16),
            pltpu.VMEM((n_z, 8, pos), F32),
            pltpu.VMEM((n_z, micro, n_q, cw, pos), BF16),
            pltpu.VMEM((n_z, micro, n_q, cw, pos), BF16),
            pltpu.VMEM((n_z, 8, pos), F32),
            pltpu.VMEM((rows, pos), F32),
            pltpu.VMEM((2, n_q, n_d, rows, pos), F32),
            pltpu.VMEM((rows, pos), F32),
            pltpu.VMEM((2, n_z, rows, pos), F32),
            pltpu.VMEM((rows, pos), F32),
            pltpu.VMEM((n_q, cw, pos), F32),
            pltpu.VMEM((3, cw, pos), F32),
            pltpu.VMEM((cw, length, pos), BF16),
            pltpu.VMEM((n_z, rows * cw, pos), F32),
            pltpu.VMEM((rows * cw, pos), F32),
            pltpu.VMEM((n_z, rows * cw, pos), F32),
            dma(n_q), dma(n_q), dma(n_z), dma(n_z), dma(n_z), dma(n_z),
            dma(n_z, n_q), dma(n_z, n_q),
            dma(2, n_q, n_d), dma(2, n_q, n_d), dma(2, n_z), dma(2, n_z),
            dma(n_z, n_q), dma(n_z, n_q), dma(n_z, n_q), dma(n_z, n_q),
            dma(2, n_q), dma(2, n_z, n_q), dma(4),
        ],
        compiler_params=pltpu.CompilerParams(
            collective_id=0, has_side_effects=True, vmem_limit_bytes=40 * 1024 * 1024
        ),
    )(inp, fil, cot, par)
    grads = gout[:, :, :2, :cw].transpose(2, 1, 0, 3).reshape(2, channels)
    return out.reshape(1, micro, channels, pos), grads[None]


def solution(mesh):
    return jax.shard_map(
        local,
        mesh=mesh,
        in_specs=(
            P(None, "dp", "seq"),
            P("section", "dp", "seq", None),
            P("section", "dp"),
            P("section", "dp"),
            P("section", "dp"),
            P("section", None, "dp", "seq"),
        ),
        out_specs=(P("section", None, "dp", "seq"), P("section", None, "dp")),
        check_vma=False,
    )
```
